32 devices in a mesh: slab: 4 (over y, x), leaf: 8 (over z, core).
Axes of the slice: x: 2, y: 2, z: 4, core: 2. Of those that a mesh axis runs over, the one named last changes fastest.
Arguments:
- right_sides: bfloat16 [32, 131072], P(None, ('slab', 'leaf')), may hold values from -6 to 6
- left_sides: bfloat16 [32, 131072], P(None, ('slab', 'leaf')), may hold values from -6 to 6
- near_blocks: bfloat16 [1024, 8, 128, 128], P(('slab', 'leaf')), may hold values from -0.1875 to 0.1875
- near_columns: int32 [1024, 8], P(('slab', 'leaf')), may hold values from 0 to 1023, as said below
- cluster_points: int32 [1024], P(('slab', 'leaf')), may hold values from 64 to 128, as said below
- leaf_basis: bfloat16 [1024, 64, 128], P(('slab', 'leaf')), may hold values from -0.5 to 0.5
- transfer: float32 [1024, 64, 128], P(('slab', 'leaf')), may hold values from -0.625 to 0.625
- far_parents: int32 [32, 24], P(('slab', 'leaf')), may hold values from 0 to 31, as said below
- far_count: int32 [32], P(('slab', 'leaf')), may hold values from 12 to 24, as said below
- coupling: float32 [32, 24, 128, 128], P(('slab', 'leaf')), may hold values from -0.375 to 0.375
- slab_transfer: float32 [32, 128, 128], P(('slab', 'leaf')), may hold values from -0.75 to 0.75
- apex_coupling: float32 [4, 4, 128, 128], replicated, may hold values from -0.75 to 0.75
Outputs:
- product: float32 [32, 131072], P(None, ('slab', 'leaf'))
- adjoint_product: float32 [32, 131072], P(None, ('slab', 'leaf'))
The draws below stay inside these ranges and needn't reach their ends.
Inputs may be any that keep to these rules, and one draw needn't show every extreme that they name: `near_columns`: row i holds 8 different clusters, i among them, all inside the window of 9 consecutive clusters centred on i, moved inward where it would pass an end of 0 to 1023. `cluster_points`: some cluster has exactly 128 points and some exactly 64. `far_parents`: row p holds 24 different parents, none equal to p; only the first far_count[p] are used. `far_count`: some parent uses all 24 slots and some exactly 12.
All inputs are finite; a program needn't handle non-finite values.
Results may differ from the reference program's by a relative error of at most 0.0024.
Values may be sent and summed in bfloat16 or wider, within the bound.
A program may use at most 128 MiB of HBM per device.

```python
import jax
import jax.numpy as jnp
from jax import lax

B = 128
R = 32
K = 64
K2 = 128
K3 = 128
NN = 8
HW = 4
CL = 32
PARENTS = 32
NF = 24
SLABS = 4
PER_SLAB = 8
NC = 1024
N = 131072


def draw_near_columns(key, part):
    window = 2 * HW + 1
    row_index = jnp.arange(NC, dtype=jnp.int32)
    window_start = jnp.clip(row_index - HW, 0, NC - window)
    scores = jax.random.randint(key, (NC, window), 0, 1 << 16, dtype=jnp.int32) * window + jnp.arange(window, dtype=jnp.int32)[None, :]
    own_slot = (row_index - window_start)[:, None] == jnp.arange(window, dtype=jnp.int32)[None, :]
    scores = jnp.where(own_slot, -1, scores)
    ranking = jnp.argsort(scores, axis=1)[:, :NN].astype(jnp.int32)
    return (window_start[:, None] + ranking).astype(jnp.int32)


def draw_cluster_points(key, part):
    values = jax.random.randint(key, (NC,), B // 2, B + 1, dtype=jnp.int32)
    top_slot = jax.random.randint(jax.random.fold_in(key, 1), (), 0, NC, dtype=jnp.int32)
    low_slot = (top_slot + 1) % NC
    return values.at[top_slot].set(B).at[low_slot].set(B // 2).astype(jnp.int32)


def draw_far_parents(key, part):
    scores = jax.random.randint(key, (PARENTS, PARENTS), 0, 1 << 20, dtype=jnp.int32) * PARENTS + jnp.arange(PARENTS, dtype=jnp.int32)[None, :]
    scores = jnp.where(jnp.eye(PARENTS, dtype=jnp.bool_), 1 << 30, scores)
    return jnp.argsort(scores, axis=1)[:, :NF].astype(jnp.int32)


def draw_far_count(key, part):
    values = jax.random.randint(key, (PARENTS,), NF // 2, NF + 1, dtype=jnp.int32)
    top_slot = jax.random.randint(jax.random.fold_in(key, 2), (), 0, PARENTS, dtype=jnp.int32)
    low_slot = (top_slot + 1) % PARENTS
    return values.at[top_slot].set(NF).at[low_slot].set(NF // 2).astype(jnp.int32)


def level_of(stream_key, dims, cuts, smallest, high):
    def one(axis_at, shards_of):
        heights = jax.random.uniform(jax.random.fold_in(jax.random.fold_in(stream_key, 6), axis_at), (shards_of,), jnp.float32, smallest / len(cuts), high / len(cuts))
        return jnp.repeat(jnp.exp(heights), dims[axis_at] // shards_of).reshape((-1,) + (1,) * (len(dims) - axis_at - 1))

    gain = one(*cuts[0])
    for cut in cuts[1:]:
        gain = gain * one(*cut)
    return gain


def noise(stream_key, dims, scale, most, cuts=(), kind=jnp.bfloat16):
    gain = level_of(stream_key, dims, cuts, -0.22, 0.18) if cuts else 1.0
    array = jax.random.normal(stream_key, dims, jnp.float32) * scale * gain
    return jnp.minimum(jnp.maximum(array, -most), most).astype(kind)


def setup_inputs(seed: int = 0) -> dict:
    seeds = jax.random.split(jax.random.key(seed), 13)
    return {
        "right_sides": noise(seeds[0], (R, N), 1.0, 6.0, ((1, 32),)),
        "left_sides": noise(seeds[1], (R, N), 1.0, 6.0, ((1, 32),)),
        "near_blocks": noise(seeds[2], (NC, NN, B, B), (B * NN) ** -0.5, 0.1875, ((0, 32),)),
        "near_columns": draw_near_columns(jax.random.fold_in(seeds[12], 71), 0),
        "cluster_points": draw_cluster_points(jax.random.fold_in(seeds[12], 71), 0),
        "leaf_basis": noise(seeds[5], (NC, K, B), B ** -0.5, 0.5, ((0, 32),)),
        "transfer": noise(seeds[6], (NC, K, K2), ((CL * K * K2) ** -0.25), 0.625, ((0, 32),), jnp.float32),
        "far_parents": draw_far_parents(jax.random.fold_in(seeds[12], 71), 0),
        "far_count": draw_far_count(jax.random.fold_in(seeds[12], 71), 0),
        "coupling": noise(seeds[9], (PARENTS, NF, K2, K2), ((NF * K2 // 2) ** -0.5), 0.375, ((0, 32),), jnp.float32),
        "slab_transfer": noise(seeds[10], (PARENTS, K2, K3), ((PER_SLAB * K2 * K3) ** -0.25), 0.75, ((0, 32),), jnp.float32),
        "apex_coupling": noise(seeds[11], (SLABS, SLABS, K3, K3), (((SLABS - 1) * K3) ** -0.5), 0.75, (), jnp.float32),
    }


def reference(right_sides, left_sides, near_blocks, near_columns, cluster_points, leaf_basis, transfer, far_parents, far_count, coupling, slab_transfer, apex_coupling):
    uppermost_level = lax.Precision.HIGHEST
    point_mask = jnp.arange(B, dtype=jnp.int32)[None, :] < cluster_points[:, None]
    zero_bf = jnp.zeros((), jnp.bfloat16)
    masked_right = jnp.where(point_mask[None], right_sides.reshape(R, NC, B), zero_bf)
    masked_left = jnp.where(point_mask[None], left_sides.reshape(R, NC, B), zero_bf)
    group_blocks = near_blocks.reshape(PARENTS, CL, NN, B, B)
    group_columns = near_columns.reshape(PARENTS, CL, NN)
    group_left = jnp.transpose(masked_left.reshape(R, PARENTS, CL, B), (1, 0, 2, 3))

    def near_forward(pieces):
        blocks, columns = pieces
        picked = jnp.take(masked_right, columns, axis=1).astype(jnp.float32)
        return jnp.einsum("csab,rcsb->rca", blocks.astype(jnp.float32), picked, precision=uppermost_level)

    near_out = lax.map(near_forward, (group_blocks, group_columns))
    near_out = jnp.transpose(near_out, (1, 0, 2, 3)).reshape(R, NC, B)

    def near_transposed(total, pieces):
        blocks, columns, lefts = pieces
        contrib = jnp.einsum("csab,rca->csrb", blocks.astype(jnp.float32), lefts.astype(jnp.float32), precision=uppermost_level)
        total = total.at[columns.reshape(-1)].add(contrib.reshape(CL * NN, R, B))
        return total, None

    near_back, _ = lax.scan(near_transposed, jnp.zeros((NC, R, B), jnp.float32), (group_blocks, group_columns, group_left))
    near_back = jnp.transpose(near_back, (1, 0, 2))

    basis_wide = leaf_basis.astype(jnp.float32)
    leaf_right = jnp.einsum("ckb,rcb->ckr", basis_wide, masked_right.astype(jnp.float32), precision=uppermost_level)
    leaf_left = jnp.einsum("ckb,rcb->ckr", basis_wide, masked_left.astype(jnp.float32), precision=uppermost_level)
    parent_right = jnp.einsum("ckq,ckr->cqr", transfer, leaf_right, precision=uppermost_level).reshape(PARENTS, CL, K2, R).sum(axis=1)
    parent_left = jnp.einsum("ckq,ckr->cqr", transfer, leaf_left, precision=uppermost_level).reshape(PARENTS, CL, K2, R).sum(axis=1)

    live = (jnp.arange(NF, dtype=jnp.int32)[None, :] < far_count[:, None]).astype(jnp.float32)
    far_right = jnp.einsum("pf,pfab,pfbr->par", live, coupling, parent_right[far_parents], precision=uppermost_level)
    outward = jnp.einsum("pf,pfab,par->pfbr", live, coupling, parent_left, precision=uppermost_level)
    far_left = jnp.zeros((PARENTS, K2, R), jnp.float32).at[far_parents.reshape(-1)].add(outward.reshape(PARENTS * NF, K2, R))

    slab_right = jnp.einsum("pqt,pqr->ptr", slab_transfer, parent_right, precision=uppermost_level).reshape(SLABS, PER_SLAB, K3, R).sum(axis=1)
    slab_left_factor = jnp.einsum("pqt,pqr->ptr", slab_transfer, parent_left, precision=uppermost_level).reshape(SLABS, PER_SLAB, K3, R).sum(axis=1)
    remaining_slabs = 1.0 - jnp.eye(SLABS, dtype=jnp.float32)
    apex_right = jnp.einsum("st,stab,tbr->sar", remaining_slabs, apex_coupling, slab_right, precision=uppermost_level)
    apex_left = jnp.einsum("uc,ucnh,unx->chx", remaining_slabs, apex_coupling, slab_left_factor, precision=uppermost_level)
    hat_right = far_right + jnp.einsum("pqt,ptr->pqr", slab_transfer, jnp.repeat(apex_right, PER_SLAB, axis=0), precision=uppermost_level)
    hat_left = far_left + jnp.einsum("pqt,ptr->pqr", slab_transfer, jnp.repeat(apex_left, PER_SLAB, axis=0), precision=uppermost_level)

    down_right = jnp.einsum("ckq,cqr->ckr", transfer, jnp.repeat(hat_right, CL, axis=0), precision=uppermost_level).astype(jnp.bfloat16)
    down_left = jnp.einsum("ckq,cqr->ckr", transfer, jnp.repeat(hat_left, CL, axis=0), precision=uppermost_level).astype(jnp.bfloat16)
    far_out = jnp.einsum("ckb,ckr->rcb", basis_wide, down_right.astype(jnp.float32), precision=uppermost_level)
    far_back = jnp.einsum("ckb,ckr->rcb", basis_wide, down_left.astype(jnp.float32), precision=uppermost_level)
    zero_wide = jnp.zeros((), jnp.float32)
    product = jnp.where(point_mask[None], near_out + far_out, zero_wide).reshape(R, N)
    adjoint_product = jnp.where(point_mask[None], near_back + far_back, zero_wide).reshape(R, N)
    return product, adjoint_product
```

```python
import functools

import jax
import jax.numpy as jnp
from jax import lax
from jax.experimental import pallas as pl
from jax.experimental.pallas import tpu as pltpu
from jax.sharding import PartitionSpec as P

B = 128
HW = 4
CORES = 2
BF = jnp.bfloat16
F32 = jnp.float32
MESH = pl.DeviceIdType.MESH


def nt(a, b):
    return lax.dot_general(a, b, (((1,), (1,)), ((), ())), preferred_element_type=F32)


def nn(a, b):
    return lax.dot_general(a, b, (((1,), (0,)), ((), ())), preferred_element_type=F32)


def split(x):
    high = x.astype(BF)
    return high, (x - high.astype(F32)).astype(BF)


def stacked(x):
    return jnp.concatenate(split(x), axis=0)


def wide(x):
    return jnp.concatenate(split(x), axis=1)


def three_nn(a, pair):
    rows, columns = a.shape[0], pair.shape[1] // 2
    both = nn(stacked(a), pair)
    return both[:rows, :columns] + both[rows:, :columns] + both[:rows, columns:]


def paired_rows(a):
    high, low = split(a)
    return jnp.concatenate(
        [
            jnp.concatenate([high, high], axis=1),
            jnp.concatenate([low, jnp.zeros_like(low)], axis=1),
        ],
        axis=0,
    )


def three_nt(a, pair):
    rows = a.shape[0]
    both = nt(paired_rows(a), pair)
    return both[:rows] + both[rows:]


def kernel(
    slabs,
    leaves,
    count_s,
    points_h,
    targets_h,
    columns_h,
    right_h,
    left_h,
    basis_h,
    transfer_h,
    lift_h,
    coupling_h,
    apex_h,
    near_h,
    product_ref,
    adjoint_ref,
    right_v,
    left_v,
    basis_v,
    transfer_v,
    lift_v,
    coupling_v,
    apex_v,
    near_v,
    columns_v,
    table_v,
    far_table_v,
    points_s,
    targets_s,
    table_s,
    far_table_s,
    ext_v,
    masked_left_v,
    leaf_v,
    transfer2_v,
    lift2_v,
    coupling2_v,
    apex2_v,
    collected_v,
    near_out_v,
    edge_out_v,
    edge_in_v,
    share_v,
    share_in_v,
    slab_v,
    top_v,
    parents_v,
    terms_v,
    core_out_v,
    core_in_v,
    slab_out_v,
    slab_in_v,
    own_v,
    chip_out_v,
    chip_in_v,
    in_sem,
    table_sem,
    halo_send,
    halo_recv,
    edge_send,
    edge_recv,
    share_send,
    share_recv,
    slab_send,
    slab_recv,
    top_send,
    top_recv,
    pchip_send,
    pchip_recv,
    pslab_send,
    pslab_recv,
    ochip_send,
    ochip_recv,
    oslab_send,
    oslab_recv,
    core_send,
    core_recv,
):
    rhs = right_h.shape[0]
    slots, clusters = columns_v.shape
    rank = leaf_v.shape[1] // clusters
    pack = B // rank
    far_slots = coupling_v.shape[0]
    devices = slabs * leaves
    chips = leaves // CORES
    group = slabs * chips
    width = 2 * HW + 1
    chunk = share_v.shape[1]
    my_slab = lax.axis_index("slab")
    my_leaf = lax.axis_index("leaf")
    my_chip = my_leaf // CORES
    my_core = my_leaf % CORES
    me = my_slab * leaves + my_leaf
    first = 1 - (me + devices - 1) // devices
    last = (me + 1) // devices
    is_right = my_leaf * chunk < rhs

    def place(d):
        return (d // leaves, d % leaves)

    def loop(low, high, act):
        def step(k, carry):
            act(k)
            return carry

        lax.fori_loop(low, high, step, 0)

    inputs = [
        pltpu.make_async_copy(src, dst, in_sem.at[i])
        for i, (src, dst) in enumerate(
            [
                (right_h, right_v),
                (left_h, left_v),
                (basis_h, basis_v),
                (transfer_h, transfer_v),
                (lift_h, lift_v),
                (coupling_h, coupling_v),
                (near_h, near_v.at[pl.ds(0, clusters * slots)]),
                (columns_h, columns_v),
                (points_h, points_s),
                (targets_h, targets_s),
            ]
        )
    ]
    apex_row = pltpu.make_async_copy(apex_h.at[my_slab], apex_v, in_sem.at[10])
    apex_column = pltpu.make_async_copy(apex_h.at[:, my_slab], apex_v, in_sem.at[10])
    for copy in inputs[7:] + inputs[:7]:
        copy.start()

    @pl.when(is_right)
    def _():
        apex_row.start()

    @pl.when(jnp.logical_not(is_right))
    def _():
        apex_column.start()

    ext_v[0:HW] = jnp.zeros((HW, rhs, B), BF)
    ext_v[clusters + HW :] = jnp.zeros((HW, rhs, B), BF)
    edge_in_v[...] = jnp.zeros_like(edge_in_v)
    slab_in_v[my_slab] = jnp.zeros(slab_in_v.shape[1:], BF)
    chip_in_v[my_chip] = jnp.zeros(chip_in_v.shape[1:], BF)
    parents_v[CORES * group] = jnp.zeros(parents_v.shape[1:], BF)

    barrier = pltpu.get_barrier_semaphore()

    def greet(slab, leaf):
        pl.semaphore_signal(barrier, inc=1, device_id=(slab, leaf), device_id_type=MESH)

    loop(1, leaves, lambda k: greet(my_slab, (my_leaf + k) % leaves))
    loop(1, slabs, lambda k: greet((my_slab + k) % slabs, my_leaf))
    after = jnp.where(my_leaf == leaves - 1, jnp.where(my_slab < slabs - 1, 1, 0), 0)
    before = jnp.where(my_leaf == 0, jnp.where(my_slab > 0, 1, 0), 0)

    @pl.when(after == 1)
    def _():
        greet(my_slab + 1, 0)

    @pl.when(before == 1)
    def _():
        greet(my_slab - 1, leaves - 1)

    collected_v[...] = jnp.zeros_like(collected_v)
    near_v[clusters * slots] = jnp.zeros((B, B), BF)
    terms_v[far_slots] = jnp.zeros(terms_v.shape[1:], F32)

    for copy in inputs[7:]:
        copy.wait()
    row = lax.broadcasted_iota(jnp.int32, (1, clusters), 1)
    opening = (
        row
        + first * jnp.maximum(HW - row, 0)
        - last * jnp.maximum(row - (clusters - HW - 1), 0)
    )
    spots = [columns_v[s : s + 1] - (me * clusters - HW) for s in range(slots)]
    for w in range(width):
        found = jnp.full((1, clusters), clusters * slots, jnp.int32)
        for s in range(slots):
            found = jnp.where(spots[s] == opening + w, row * slots + s, found)
        table_v[w : w + 1] = found
    for s in range(slots):
        table_v[width + s : width + s + 1] = jnp.clip(spots[s], 0, clusters + 2 * HW - 1)
    owner = lax.broadcasted_iota(jnp.int32, (1, devices), 1)
    found = jnp.full((1, devices), far_slots, jnp.int32)
    for f in range(far_slots):
        target = jnp.where(f < count_s[0], targets_s[f], -1)
        found = jnp.where(owner == target, f, found)
    far_table_v[0:1] = found
    tables = [
        pltpu.make_async_copy(table_v, table_s, table_sem.at[0]),
        pltpu.make_async_copy(far_table_v, far_table_s, table_sem.at[1]),
    ]
    for copy in tables:
        copy.start()

    lane = lax.broadcasted_iota(jnp.int32, (rhs, B), 1)
    lane2 = lax.broadcasted_iota(jnp.int32, (2 * rhs, B), 1)

    for copy in inputs[:3]:
        copy.wait()

    def leaf_step(g):
        rows = []
        for u in range(pack):
            c = g * pack + u
            window = slice(c * B, (c + 1) * B)
            mask = jnp.where(lane < points_s[c], 1.0, 0.0).astype(BF)
            r = right_v[:, window] * mask
            l = left_v[:, window] * mask
            ext_v[c + HW] = r
            masked_left_v[c] = l
            rows += [r, l]
        both = nt(jnp.concatenate(rows, axis=0), basis_v[g])
        leaf = both[: 2 * rhs]
        for u in range(1, pack):
            leaf = jnp.where(lane2 < u * rank, leaf, both[2 * rhs * u : 2 * rhs * (u + 1)])
        high, low = split(leaf)
        leaf_v[: 2 * rhs, g * B : (g + 1) * B] = high
        leaf_v[2 * rhs :, g * B : (g + 1) * B] = low

    for g in range(clusters // pack):
        leaf_step(g)
    inputs[3].wait()
    inputs[4].wait()
    transfer2_v[...] = wide(transfer_v[...])
    lift2_v[...] = wide(lift_v[...])
    both = nn(leaf_v[...], transfer2_v[...])
    k2 = transfer_v.shape[1]
    parent = both[: 2 * rhs, :k2] + both[2 * rhs :, :k2] + both[: 2 * rhs, k2:]

    def spot(slab, leaf):
        return (leaf % CORES) * group + slab * chips + leaf // CORES

    parents_v[spot(my_slab, my_leaf)] = parent[:rhs].astype(BF)
    share = three_nn(parent, lift2_v[...])
    for j in range(leaves):
        share_v[j] = share[j * chunk : (j + 1) * chunk]

    pl.semaphore_wait(barrier, leaves - 1 + slabs - 1 + after + before)

    def remote(src, dst, send, recv, device):
        return pltpu.make_async_remote_copy(
            src_ref=src,
            dst_ref=dst,
            send_sem=send,
            recv_sem=recv,
            device_id=device,
            device_id_type=MESH,
        )

    def share_copy(k):
        peer = (my_leaf + k) % leaves
        return remote(
            share_v.at[peer],
            share_in_v.at[my_leaf],
            share_send.at[k],
            share_recv.at[k],
            (my_slab, peer),
        )

    def share_arrival(k):
        peer = (my_leaf + leaves - k) % leaves
        return remote(
            share_v.at[my_leaf],
            share_in_v.at[peer],
            share_send.at[k],
            share_recv.at[k],
            (my_slab, peer),
        )

    def slab_copy(k):
        return remote(
            slab_v.at[my_slab],
            slab_v.at[my_slab],
            slab_send.at[k],
            slab_recv.at[k],
            ((my_slab + k) % slabs, my_leaf),
        )

    def slab_arrival(k):
        peer = (my_slab + slabs - k) % slabs
        return remote(
            slab_v.at[my_slab],
            slab_v.at[peer],
            slab_send.at[k],
            slab_recv.at[k],
            (peer, my_leaf),
        )

    def top_copy(k):
        return remote(
            top_v.at[my_leaf],
            top_v.at[my_leaf],
            top_send.at[k],
            top_recv.at[k],
            (my_slab, (my_leaf + k) % leaves),
        )

    def top_arrival(k):
        peer = (my_leaf + leaves - k) % leaves
        return remote(
            top_v.at[my_leaf],
            top_v.at[peer],
            top_send.at[k],
            top_recv.at[k],
            (my_slab, peer),
        )

    def chip_leaf(k):
        return ((my_chip + k) % chips) * CORES + my_core

    def parent_chip_copy(k):
        at = spot(my_slab, my_leaf)
        return remote(
            parents_v.at[at],
            parents_v.at[at],
            pchip_send.at[k],
            pchip_recv.at[k],
            (my_slab, chip_leaf(k)),
        )

    def parent_chip_arrival(k):
        leaf = chip_leaf(chips - k)
        return remote(
            parents_v.at[spot(my_slab, my_leaf)],
            parents_v.at[spot(my_slab, leaf)],
            pchip_send.at[k],
            pchip_recv.at[k],
            (my_slab, leaf),
        )

    def column(core, slab):
        return parents_v.at[pl.ds(core * group + slab * chips, chips)]

    def parent_slab_copy(k):
        return remote(
            column(my_core, my_slab),
            column(my_core, my_slab),
            pslab_send.at[k],
            pslab_recv.at[k],
            ((my_slab + k) % slabs, my_leaf),
        )

    def parent_slab_arrival(k):
        peer = (my_slab + slabs - k) % slabs
        return remote(
            column(my_core, my_slab),
            column(my_core, peer),
            pslab_send.at[k],
            pslab_recv.at[k],
            (peer, my_leaf),
        )

    partner = (my_slab, my_chip * CORES + 1 - my_core)

    def parent_core_copy():
        half = parents_v.at[pl.ds(my_core * group, group)]
        return remote(half, half, core_send.at[0], core_recv.at[0], partner)

    def parent_core_arrival():
        half = parents_v.at[pl.ds(my_core * group, group)]
        other = parents_v.at[pl.ds((1 - my_core) * group, group)]
        return remote(half, other, core_send.at[0], core_recv.at[0], partner)

    def outward_core_copy():
        return remote(core_out_v, core_in_v, core_send.at[1], core_recv.at[1], partner)

    def outward_slab_copy(k):
        peer = (my_slab + k) % slabs
        return remote(
            slab_out_v.at[peer],
            slab_in_v.at[my_slab],
            oslab_send.at[k],
            oslab_recv.at[k],
            (peer, my_leaf),
        )

    def outward_slab_arrival(k):
        peer = (my_slab + slabs - k) % slabs
        return remote(
            slab_out_v.at[my_slab],
            slab_in_v.at[peer],
            oslab_send.at[k],
            oslab_recv.at[k],
            (peer, my_leaf),
        )

    def outward_chip_copy(k):
        peer = (my_chip + k) % chips
        return remote(
            chip_out_v.at[peer],
            chip_in_v.at[my_chip],
            ochip_send.at[k],
            ochip_recv.at[k],
            (my_slab, chip_leaf(k)),
        )

    def outward_chip_arrival(k):
        peer = (my_chip + chips - k) % chips
        return remote(
            chip_out_v.at[my_chip],
            chip_in_v.at[peer],
            ochip_send.at[k],
            ochip_recv.at[k],
            (my_slab, chip_leaf(chips - k)),
        )

    def halo_copy(to_next):
        where = me + 1 if to_next else me - 1
        src = clusters if to_next else HW
        dst = 0 if to_next else clusters + HW
        i = 0 if to_next else 1
        return remote(
            ext_v.at[pl.ds(src, HW)],
            ext_v.at[pl.ds(dst, HW)],
            halo_send.at[i],
            halo_recv.at[i],
            place(where),
        )

    def edge_copy(to_next):
        i = 1 if to_next else 0
        return remote(
            edge_out_v.at[i],
            edge_in_v.at[i],
            edge_send.at[i],
            edge_recv.at[i],
            place(me + 1 if to_next else me - 1),
        )

    loop(1, leaves, lambda k: share_copy(k).start())
    loop(1, chips, lambda k: parent_chip_copy(k).start())
    share_in_v[my_leaf] = share_v[my_leaf]

    @pl.when(me < devices - 1)
    def _():
        halo_copy(True).start()

    @pl.when(me > 0)
    def _():
        halo_copy(False).start()

    inputs[5].wait()
    left_both = stacked(parent[rhs:])

    def term(f):
        pair = wide(coupling_v[f])
        coupling2_v[f] = pair
        both = nn(left_both, pair)
        terms_v[f] = both[:rhs, :k2] + both[rhs:, :k2] + both[:rhs, k2:]

    unroll = 4

    def term_group(g):
        for u in range(unroll):
            term(g * unroll + u)

    loop(0, far_slots // unroll, term_group)
    for copy in tables:
        copy.wait()

    def owned(slab, chip, core):
        return terms_v[far_table_s[0, slab * leaves + chip * CORES + core]]

    def core_group(slab):
        for chip in range(chips):
            core_out_v[slab * chips + chip] = owned(slab, chip, 1 - my_core)

    for slab in range(slabs):
        core_group(slab)
    outward_core_copy().start()

    apex_row.wait()
    for t in range(slabs):
        apex2_v[t] = wide(apex_v[t])

    inputs[6].wait()

    def near_back(i, e0):
        left = masked_left_v[i]
        for w in range(width):
            collected_v[e0 + w] += nn(left, near_v[table_s[w, i]])

    def near_forward(i):
        blocks = jnp.concatenate([near_v[i * slots + s] for s in range(slots)], axis=1)
        picked = jnp.concatenate([ext_v[table_s[width + s, i]] for s in range(slots)], axis=1)
        near_out_v[i] = nt(picked, blocks)

    for i in range(HW):
        near_back(i, i + first * (HW - i))
    for i in range(clusters - HW, clusters):
        near_back(i, i - last * (i - (clusters - HW - 1)))

    edge_out_v[0] = collected_v[0:HW].astype(BF)
    edge_out_v[1] = collected_v[clusters + HW :].astype(BF)

    loop(1, leaves, lambda k: share_arrival(k).wait_recv())
    total = share_in_v[0]
    for j in range(1, leaves):
        total = total + share_in_v[j]
    slab_v[my_slab] = total
    loop(1, slabs, lambda k: slab_copy(k).start())

    outward_core_copy().wait_recv()
    for slab in range(slabs):
        for chip in range(chips):
            k = slab * chips + chip
            slab_out_v[slab, chip] = (owned(slab, chip, my_core) + core_in_v[k]).astype(BF)
    loop(1, slabs, lambda k: outward_slab_copy(k).start())
    for chip in range(chips):
        own_v[chip] = owned(my_slab, chip, my_core) + core_in_v[my_slab * chips + chip]

    loop(1, chips, lambda k: parent_chip_arrival(k).wait_recv())
    loop(1, slabs, lambda k: parent_slab_copy(k).start())

    @pl.when(me < devices - 1)
    def _():
        edge_copy(True).start()

    @pl.when(me > 0)
    def _():
        edge_copy(False).start()

    def middle_back(g):
        i = HW + g * HW
        lefts = [masked_left_v[i + u] for u in range(HW)]
        for e in range(width + HW - 1):
            rows = [u for u in range(HW) if 0 <= e - u < width]
            left = jnp.concatenate([lefts[u] for u in rows], axis=1)
            blocks = jnp.concatenate([near_v[table_s[e - u, i + u]] for u in rows], axis=0)
            collected_v[i + e] += nn(left, blocks)

    middles = (clusters - 2 * HW) // HW
    loop(0, middles // 2, middle_back)

    loop(1, slabs, lambda k: slab_arrival(k).wait_recv())

    def apex_products(product):
        total = jnp.zeros((chunk, lift_v.shape[1]), F32)
        for t in range(slabs):
            other = jnp.where(my_slab == t, 0.0, 1.0)
            total += product(slab_v[t] * other, apex2_v[t])
        top_v[my_leaf] = total

    @pl.when(is_right)
    def _():
        apex_products(three_nt)

    @pl.when(jnp.logical_not(is_right))
    def _():
        apex_products(three_nn)

    loop(1, leaves, lambda k: top_copy(k).start())

    loop(1, slabs, lambda k: outward_slab_arrival(k).wait_recv())
    for chip in range(chips):
        total = own_v[chip]
        for t in range(slabs):
            total = total + slab_in_v[t, chip].astype(F32)
        own_v[chip] = total
        chip_out_v[chip] = total.astype(BF)
    loop(1, chips, lambda k: outward_chip_copy(k).start())

    loop(1, slabs, lambda k: parent_slab_arrival(k).wait_recv())
    parent_core_copy().start()

    loop(middles // 2, middles, middle_back)

    @pl.when(me > 0)
    def _():
        halo_copy(True).wait_recv()

    @pl.when(me < devices - 1)
    def _():
        halo_copy(False).wait_recv()

    def forward_group(g):
        for u in range(HW):
            near_forward(g * HW + u)

    loop(0, clusters // HW, forward_group)

    @pl.when(me > 0)
    def _():
        edge_copy(True).wait_recv()

    @pl.when(me < devices - 1)
    def _():
        edge_copy(False).wait_recv()

    collected_v[HW : 2 * HW] += edge_in_v[1].astype(F32)
    collected_v[clusters : clusters + HW] += edge_in_v[0].astype(F32)

    parent_core_arrival().wait_recv()
    batch = 4
    far_right = jnp.zeros((rhs, k2), F32)

    def far_group(g, total):
        chosen, pairs = [], []
        for u in range(batch):
            f = g * batch + u
            target = targets_s[f]
            at = spot(target // leaves, target % leaves)
            row = parents_v[jnp.where(f < count_s[0], at, CORES * group)]
            chosen += [row, row]
            pairs.append(coupling2_v[f])
        return total + nt(jnp.concatenate(chosen, axis=1), jnp.concatenate(pairs, axis=1))

    far_right = lax.fori_loop(0, far_slots // batch, far_group, far_right)

    loop(1, chips, lambda k: outward_chip_arrival(k).wait_recv())
    far_left = own_v[my_chip]
    for chip in range(chips):
        far_left = far_left + chip_in_v[chip].astype(F32)

    loop(1, leaves, lambda k: top_arrival(k).wait_recv())
    top = jnp.concatenate([top_v[j] for j in range(leaves)], axis=0)
    hat = three_nt(top, lift2_v[...]) + jnp.concatenate([far_right, far_left], axis=0)
    hat2 = paired_rows(hat)
    span = 2 * B
    for n in range(clusters * rank // span):
        both = nt(hat2, transfer2_v[n * span : (n + 1) * span])
        down = (both[: 2 * rhs] + both[2 * rhs :]).astype(BF)
        for h in range(span // B):
            g = n * (span // B) + h
            piece = down[:, h * B : (h + 1) * B]
            rows = [
                jnp.where((lane2 >= u * rank) & (lane2 < (u + 1) * rank), piece, jnp.zeros_like(piece))
                for u in range(pack)
            ]
            out = nn(jnp.concatenate(rows, axis=0), basis_v[g])
            for u in range(pack):
                c = g * pack + u
                keep = lane < points_s[c]
                base = 2 * rhs * u
                window = slice(c * B, (c + 1) * B)
                product_ref[:, window] = jnp.where(
                    keep, near_out_v[c] + out[base : base + rhs], 0.0
                )
                adjoint_ref[:, window] = jnp.where(
                    keep, collected_v[c + HW] + out[base + rhs : base + 2 * rhs], 0.0
                )

    loop(1, leaves, lambda k: share_copy(k).wait_send())
    loop(1, leaves, lambda k: top_copy(k).wait_send())
    loop(1, slabs, lambda k: slab_copy(k).wait_send())
    loop(1, slabs, lambda k: parent_slab_copy(k).wait_send())
    loop(1, slabs, lambda k: outward_slab_copy(k).wait_send())
    loop(1, chips, lambda k: parent_chip_copy(k).wait_send())
    loop(1, chips, lambda k: outward_chip_copy(k).wait_send())
    parent_core_copy().wait_send()
    outward_core_copy().wait_send()

    @pl.when(me < devices - 1)
    def _():
        halo_copy(True).wait_send()
        edge_copy(True).wait_send()

    @pl.when(me > 0)
    def _():
        halo_copy(False).wait_send()
        edge_copy(False).wait_send()


def shards(
    right_sides,
    left_sides,
    near_blocks,
    near_columns,
    cluster_points,
    leaf_basis,
    transfer,
    far_parents,
    far_count,
    coupling,
    slab_transfer,
    apex_coupling,
):
    slabs, leaves = lax.axis_size("slab"), lax.axis_size("leaf")
    devices = slabs * leaves
    chips = leaves // CORES
    group = slabs * chips
    rhs, columns = right_sides.shape
    clusters, slots = near_columns.shape
    rank, k2 = transfer.shape[1:]
    k3 = slab_transfer.shape[2]
    far_slots = coupling.shape[1]
    width = 2 * HW + 1
    chunk = 2 * rhs // leaves
    pack = B // rank
    hbm = pl.BlockSpec(memory_space=pltpu.HBM)
    vmem = pl.BlockSpec(memory_space=pltpu.VMEM)
    dma = pltpu.SemaphoreType.DMA
    out = jax.ShapeDtypeStruct((rhs, columns), F32)
    return pl.pallas_call(
        functools.partial(kernel, slabs, leaves),
        out_shape=(out, out),
        in_specs=[pl.BlockSpec(memory_space=pltpu.SMEM)] + [hbm] * 11,
        out_specs=(vmem, vmem),
        scratch_shapes=[
            pltpu.VMEM((rhs, columns), BF),
            pltpu.VMEM((rhs, columns), BF),
            pltpu.VMEM((clusters // pack, B, B), BF),
            pltpu.VMEM((clusters * rank, k2), F32),
            pltpu.VMEM((k2, k3), F32),
            pltpu.VMEM(coupling.shape[1:], F32),
            pltpu.VMEM((slabs, k3, k3), F32),
            pltpu.VMEM((clusters * slots + 1, B, B), BF),
            pltpu.VMEM((slots, clusters), jnp.int32),
            pltpu.VMEM((width + slots, clusters), jnp.int32),
            pltpu.VMEM((1, devices), jnp.int32),
            pltpu.SMEM((clusters,), jnp.int32),
            pltpu.SMEM((far_slots,), jnp.int32),
            pltpu.SMEM((width + slots, clusters), jnp.int32),
            pltpu.SMEM((1, devices), jnp.int32),
            pltpu.VMEM((clusters + 2 * HW, rhs, B), BF),
            pltpu.VMEM((clusters, rhs, B), BF),
            pltpu.VMEM((4 * rhs, clusters * rank), BF),
            pltpu.VMEM((clusters * rank, 2 * k2), BF),
            pltpu.VMEM((k2, 2 * k3), BF),
            pltpu.VMEM((far_slots, k2, 2 * k2), BF),
            pltpu.VMEM((slabs, k3, 2 * k3), BF),
            pltpu.VMEM((clusters + 2 * HW, rhs, B), F32),
            pltpu.VMEM((clusters, rhs, B), F32),
            pltpu.VMEM((2, HW, rhs, B), BF),
            pltpu.VMEM((2, HW, rhs, B), BF),
            pltpu.VMEM((leaves, chunk, k3), F32),
            pltpu.VMEM((leaves, chunk, k3), F32),
            pltpu.VMEM((slabs, chunk, k3), F32),
            pltpu.VMEM((leaves, chunk, k3), F32),
            pltpu.VMEM((CORES * group + 1, rhs, k2), BF),
            pltpu.VMEM((far_slots + 1, rhs, k2), F32),
            pltpu.VMEM((group, rhs, k2), F32),
            pltpu.VMEM((group, rhs, k2), F32),
            pltpu.VMEM((slabs, chips, rhs, k2), BF),
            pltpu.VMEM((slabs, chips, rhs, k2), BF),
            pltpu.VMEM((chips, rhs, k2), F32),
            pltpu.VMEM((chips, rhs, k2), BF),
            pltpu.VMEM((chips, rhs, k2), BF),
            dma((11,)),
            dma((2,)),
            dma((2,)),
            dma((2,)),
            dma((2,)),
            dma((2,)),
            dma((leaves,)),
            dma((leaves,)),
            dma((slabs,)),
            dma((slabs,)),
            dma((leaves,)),
            dma((leaves,)),
            dma((chips,)),
            dma((chips,)),
            dma((slabs,)),
            dma((slabs,)),
            dma((chips,)),
            dma((chips,)),
            dma((slabs,)),
            dma((slabs,)),
            dma((2,)),
            dma((2,)),
        ],
        compiler_params=pltpu.CompilerParams(
            collective_id=0, has_side_effects=True, vmem_limit_bytes=50 * 1024 * 1024
        ),
        name="h2_step",
    )(
        far_count,
        *[
            pltpu.with_memory_space_constraint(array, pltpu.HBM)
            for array in (
                cluster_points,
                far_parents[0],
                near_columns.T,
                right_sides,
                left_sides,
                leaf_basis.reshape(clusters // pack, B, B),
                transfer.reshape(clusters * rank, k2),
                slab_transfer[0],
                coupling[0],
                apex_coupling,
                near_blocks.reshape(-1, B, B),
            )
        ],
    )


def solution(mesh):
    return jax.shard_map(
        shards,
        mesh=mesh,
        in_specs=(
            P(None, ("slab", "leaf")),
            P(None, ("slab", "leaf")),
            P(("slab", "leaf"), None, None, None),
            P(("slab", "leaf"), None),
            P(("slab", "leaf")),
            P(("slab", "leaf"), None, None),
            P(("slab", "leaf"), None, None),
            P(("slab", "leaf"), None),
            P(("slab", "leaf")),
            P(("slab", "leaf"), None, None, None),
            P(("slab", "leaf"), None, None),
            P(),
        ),
        out_specs=(P(None, ("slab", "leaf")), P(None, ("slab", "leaf"))),
        check_vma=False,
    )
```

```python
import functools

import jax
import jax.numpy as jnp
from jax import lax
from jax.experimental import pallas as pl
from jax.experimental.pallas import tpu as pltpu
from jax.sharding import PartitionSpec as P

B = 128
HW = 4
CORES = 2
BF = jnp.bfloat16
F32 = jnp.float32
MESH = pl.DeviceIdType.MESH


def nt(a, b):
    return lax.dot_general(a, b, (((1,), (1,)), ((), ())), preferred_element_type=F32)


def nn(a, b):
    return lax.dot_general(a, b, (((1,), (0,)), ((), ())), preferred_element_type=F32)


def split(x):
    high = x.astype(BF)
    return high, (x - high.astype(F32)).astype(BF)


def stacked(x):
    return jnp.concatenate(split(x), axis=0)


def wide(x):
    return jnp.concatenate(split(x), axis=1)


def three_nn(a, pair):
    rows, columns = a.shape[0], pair.shape[1] // 2
    both = nn(stacked(a), pair)
    return both[:rows, :columns] + both[rows:, :columns] + both[:rows, columns:]


def paired_rows(a):
    high, low = split(a)
    return jnp.concatenate(
        [
            jnp.concatenate([high, high], axis=1),
            jnp.concatenate([low, jnp.zeros_like(low)], axis=1),
        ],
        axis=0,
    )


def three_nt(a, pair):
    rows = a.shape[0]
    both = nt(paired_rows(a), pair)
    return both[:rows] + both[rows:]


def kernel(
    slabs,
    leaves,
    count_s,
    points_h,
    targets_h,
    columns_h,
    right_h,
    left_h,
    basis_h,
    transfer_h,
    lift_h,
    coupling_h,
    apex_h,
    near_h,
    hat_ref,
    near_out_v,
    collected_v,
    transfer2_v,
    basis_v,
    keep_v,
    right_v,
    left_v,
    transfer_v,
    lift_v,
    coupling_v,
    apex_v,
    near_v,
    columns_v,
    table_v,
    far_table_v,
    points_s,
    targets_s,
    table_s,
    far_table_s,
    ext_v,
    masked_left_v,
    leaf_v,
    lift2_v,
    coupling2_v,
    apex2_v,
    edge_out_v,
    edge_in_v,
    share_v,
    share_in_v,
    slab_v,
    top_v,
    parents_v,
    terms_v,
    core_out_v,
    core_in_v,
    slab_out_v,
    slab_in_v,
    own_v,
    chip_out_v,
    chip_in_v,
    in_sem,
    table_sem,
    halo_send,
    halo_recv,
    edge_send,
    edge_recv,
    share_send,
    share_recv,
    slab_send,
    slab_recv,
    top_send,
    top_recv,
    pchip_send,
    pchip_recv,
    pslab_send,
    pslab_recv,
    ochip_send,
    ochip_recv,
    oslab_send,
    oslab_recv,
    core_send,
    core_recv,
):
    rhs = right_h.shape[0]
    slots, clusters = columns_v.shape
    rank = leaf_v.shape[1] // clusters
    pack = B // rank
    far_slots = coupling_v.shape[0]
    devices = slabs * leaves
    chips = leaves // CORES
    group = slabs * chips
    width = 2 * HW + 1
    chunk = share_v.shape[1]
    my_slab = lax.axis_index("slab")
    my_leaf = lax.axis_index("leaf")
    my_chip = my_leaf // CORES
    my_core = my_leaf % CORES
    me = my_slab * leaves + my_leaf
    first = 1 - (me + devices - 1) // devices
    last = (me + 1) // devices
    is_right = my_leaf * chunk < rhs

    def place(d):
        return (d // leaves, d % leaves)

    def loop(low, high, act):
        def step(k, carry):
            act(k)
            return carry

        lax.fori_loop(low, high, step, 0)

    inputs = [
        pltpu.make_async_copy(src, dst, in_sem.at[i])
        for i, (src, dst) in enumerate(
            [
                (right_h, right_v),
                (left_h, left_v),
                (basis_h, basis_v),
                (transfer_h, transfer_v),
                (lift_h, lift_v),
                (coupling_h, coupling_v),
                (near_h, near_v.at[pl.ds(0, clusters * slots)]),
                (columns_h, columns_v),
                (points_h, points_s),
                (targets_h, targets_s),
            ]
        )
    ]
    apex_row = pltpu.make_async_copy(apex_h.at[my_slab], apex_v, in_sem.at[10])
    apex_column = pltpu.make_async_copy(apex_h.at[:, my_slab], apex_v, in_sem.at[10])
    for copy in inputs[7:] + inputs[:6]:
        copy.start()

    @pl.when(is_right)
    def _():
        apex_row.start()

    @pl.when(jnp.logical_not(is_right))
    def _():
        apex_column.start()

    ext_v[0:HW] = jnp.zeros((HW, rhs, B), BF)
    ext_v[clusters + HW :] = jnp.zeros((HW, rhs, B), BF)
    edge_in_v[...] = jnp.zeros_like(edge_in_v)
    slab_in_v[my_slab] = jnp.zeros(slab_in_v.shape[1:], BF)
    chip_in_v[my_chip] = jnp.zeros(chip_in_v.shape[1:], BF)
    parents_v[CORES * group] = jnp.zeros(parents_v.shape[1:], BF)

    barrier = pltpu.get_barrier_semaphore()

    def greet(slab, leaf):
        pl.semaphore_signal(barrier, inc=1, device_id=(slab, leaf), device_id_type=MESH)

    loop(1, leaves, lambda k: greet(my_slab, (my_leaf + k) % leaves))
    loop(1, slabs, lambda k: greet((my_slab + k) % slabs, my_leaf))
    after = jnp.where(my_leaf == leaves - 1, jnp.where(my_slab < slabs - 1, 1, 0), 0)
    before = jnp.where(my_leaf == 0, jnp.where(my_slab > 0, 1, 0), 0)

    @pl.when(after == 1)
    def _():
        greet(my_slab + 1, 0)

    @pl.when(before == 1)
    def _():
        greet(my_slab - 1, leaves - 1)

    lane = lax.broadcasted_iota(jnp.int32, (rhs, B), 1)
    lane2 = lax.broadcasted_iota(jnp.int32, (2 * rhs, B), 1)

    for copy in inputs[8:] + inputs[:4]:
        copy.wait()

    def leaf_step(g):
        rows = []
        for u in range(pack):
            c = g * pack + u
            window = slice(c * B, (c + 1) * B)
            mask = jnp.where(lane < points_s[c], 1.0, 0.0).astype(BF)
            keep_v[c : c + 1] = jnp.where(lane[:1] < points_s[c], 1.0, 0.0)
            r = right_v[:, window] * mask
            l = left_v[:, window] * mask
            ext_v[c + HW] = r
            masked_left_v[c] = l
            rows += [r, l]
        both = nt(jnp.concatenate(rows, axis=0), basis_v[g])
        leaf = both[: 2 * rhs]
        for u in range(1, pack):
            leaf = jnp.where(lane2 < u * rank, leaf, both[2 * rhs * u : 2 * rhs * (u + 1)])
        high, low = split(leaf)
        leaf_v[: 2 * rhs, g * B : (g + 1) * B] = high
        leaf_v[2 * rhs :, g * B : (g + 1) * B] = low

    inputs[6].start()
    for g in range(clusters // pack):
        leaf_step(g)
    inputs[4].wait()
    transfer2_v[...] = wide(transfer_v[...])
    lift2_v[...] = wide(lift_v[...])
    both = nn(leaf_v[...], transfer2_v[...])
    k2 = transfer_v.shape[1]
    parent = both[: 2 * rhs, :k2] + both[2 * rhs :, :k2] + both[: 2 * rhs, k2:]

    def spot(slab, leaf):
        return (leaf % CORES) * group + slab * chips + leaf // CORES

    parents_v[spot(my_slab, my_leaf)] = parent[:rhs].astype(BF)
    share = three_nn(parent, lift2_v[...])
    for j in range(leaves):
        share_v[j] = share[j * chunk : (j + 1) * chunk]

    pl.semaphore_wait(barrier, leaves - 1 + slabs - 1 + after + before)

    def remote(src, dst, send, recv, device):
        return pltpu.make_async_remote_copy(
            src_ref=src,
            dst_ref=dst,
            send_sem=send,
            recv_sem=recv,
            device_id=device,
            device_id_type=MESH,
        )

    def share_copy(k):
        peer = (my_leaf + k) % leaves
        return remote(
            share_v.at[peer],
            share_in_v.at[my_leaf],
            share_send.at[k],
            share_recv.at[k],
            (my_slab, peer),
        )

    def share_arrival(k):
        peer = (my_leaf + leaves - k) % leaves
        return remote(
            share_v.at[my_leaf],
            share_in_v.at[peer],
            share_send.at[k],
            share_recv.at[k],
            (my_slab, peer),
        )

    def slab_copy(k):
        return remote(
            slab_v.at[my_slab],
            slab_v.at[my_slab],
            slab_send.at[k],
            slab_recv.at[k],
            ((my_slab + k) % slabs, my_leaf),
        )

    def slab_arrival(k):
        peer = (my_slab + slabs - k) % slabs
        return remote(
            slab_v.at[my_slab],
            slab_v.at[peer],
            slab_send.at[k],
            slab_recv.at[k],
            (peer, my_leaf),
        )

    def top_copy(k):
        return remote(
            top_v.at[my_leaf],
            top_v.at[my_leaf],
            top_send.at[k],
            top_recv.at[k],
            (my_slab, (my_leaf + k) % leaves),
        )

    def top_arrival(k):
        peer = (my_leaf + leaves - k) % leaves
        return remote(
            top_v.at[my_leaf],
            top_v.at[peer],
            top_send.at[k],
            top_recv.at[k],
            (my_slab, peer),
        )

    def chip_leaf(k):
        return ((my_chip + k) % chips) * CORES + my_core

    def parent_chip_copy(k):
        at = spot(my_slab, my_leaf)
        return remote(
            parents_v.at[at],
            parents_v.at[at],
            pchip_send.at[k],
            pchip_recv.at[k],
            (my_slab, chip_leaf(k)),
        )

    def parent_chip_arrival(k):
        leaf = chip_leaf(chips - k)
        return remote(
            parents_v.at[spot(my_slab, my_leaf)],
            parents_v.at[spot(my_slab, leaf)],
            pchip_send.at[k],
            pchip_recv.at[k],
            (my_slab, leaf),
        )

    def column(core, slab):
        return parents_v.at[pl.ds(core * group + slab * chips, chips)]

    def parent_slab_copy(k):
        return remote(
            column(my_core, my_slab),
            column(my_core, my_slab),
            pslab_send.at[k],
            pslab_recv.at[k],
            ((my_slab + k) % slabs, my_leaf),
        )

    def parent_slab_arrival(k):
        peer = (my_slab + slabs - k) % slabs
        return remote(
            column(my_core, my_slab),
            column(my_core, peer),
            pslab_send.at[k],
            pslab_recv.at[k],
            (peer, my_leaf),
        )

    partner = (my_slab, my_chip * CORES + 1 - my_core)

    def parent_core_copy():
        half = parents_v.at[pl.ds(my_core * group, group)]
        return remote(half, half, core_send.at[0], core_recv.at[0], partner)

    def parent_core_arrival():
        half = parents_v.at[pl.ds(my_core * group, group)]
        other = parents_v.at[pl.ds((1 - my_core) * group, group)]
        return remote(half, other, core_send.at[0], core_recv.at[0], partner)

    def outward_core_copy():
        return remote(core_out_v, core_in_v, core_send.at[1], core_recv.at[1], partner)

    def outward_slab_copy(k):
        peer = (my_slab + k) % slabs
        return remote(
            slab_out_v.at[peer],
            slab_in_v.at[my_slab],
            oslab_send.at[k],
            oslab_recv.at[k],
            (peer, my_leaf),
        )

    def outward_slab_arrival(k):
        peer = (my_slab + slabs - k) % slabs
        return remote(
            slab_out_v.at[my_slab],
            slab_in_v.at[peer],
            oslab_send.at[k],
            oslab_recv.at[k],
            (peer, my_leaf),
        )

    def outward_chip_copy(k):
        peer = (my_chip + k) % chips
        return remote(
            chip_out_v.at[peer],
            chip_in_v.at[my_chip],
            ochip_send.at[k],
            ochip_recv.at[k],
            (my_slab, chip_leaf(k)),
        )

    def outward_chip_arrival(k):
        peer = (my_chip + chips - k) % chips
        return remote(
            chip_out_v.at[my_chip],
            chip_in_v.at[peer],
            ochip_send.at[k],
            ochip_recv.at[k],
            (my_slab, chip_leaf(chips - k)),
        )

    def halo_copy(to_next):
        where = me + 1 if to_next else me - 1
        src = clusters if to_next else HW
        dst = 0 if to_next else clusters + HW
        i = 0 if to_next else 1
        return remote(
            ext_v.at[pl.ds(src, HW)],
            ext_v.at[pl.ds(dst, HW)],
            halo_send.at[i],
            halo_recv.at[i],
            place(where),
        )

    def edge_copy(to_next):
        i = 1 if to_next else 0
        return remote(
            edge_out_v.at[i],
            edge_in_v.at[i],
            edge_send.at[i],
            edge_recv.at[i],
            place(me + 1 if to_next else me - 1),
        )

    loop(1, leaves, lambda k: share_copy(k).start())
    loop(1, chips, lambda k: parent_chip_copy(k).start())
    share_in_v[my_leaf] = share_v[my_leaf]

    collected_v[...] = jnp.zeros_like(collected_v)
    near_v[clusters * slots] = jnp.zeros((B, B), BF)
    terms_v[far_slots] = jnp.zeros(terms_v.shape[1:], F32)

    inputs[7].wait()
    row = lax.broadcasted_iota(jnp.int32, (1, clusters), 1)
    opening = (
        row
        + first * jnp.maximum(HW - row, 0)
        - last * jnp.maximum(row - (clusters - HW - 1), 0)
    )
    spots = [columns_v[s : s + 1] - (me * clusters - HW) for s in range(slots)]
    for w in range(width):
        found = jnp.full((1, clusters), clusters * slots, jnp.int32)
        for s in range(slots):
            found = jnp.where(spots[s] == opening + w, row * slots + s, found)
        table_v[w : w + 1] = found
    for s in range(slots):
        table_v[width + s : width + s + 1] = jnp.clip(spots[s], 0, clusters + 2 * HW - 1)
    owner = lax.broadcasted_iota(jnp.int32, (1, devices), 1)
    found = jnp.full((1, devices), far_slots, jnp.int32)
    for f in range(far_slots):
        target = jnp.where(f < count_s[0], targets_s[f], -1)
        found = jnp.where(owner == target, f, found)
    far_table_v[0:1] = found
    tables = [
        pltpu.make_async_copy(table_v, table_s, table_sem.at[0]),
        pltpu.make_async_copy(far_table_v, far_table_s, table_sem.at[1]),
    ]
    for copy in tables:
        copy.start()

    inputs[5].wait()
    left_both = stacked(parent[rhs:])

    def term(f):
        pair = wide(coupling_v[f])
        coupling2_v[f] = pair
        both = nn(left_both, pair)
        terms_v[f] = both[:rhs, :k2] + both[rhs:, :k2] + both[:rhs, k2:]

    unroll = 4

    def term_group(g):
        for u in range(unroll):
            term(g * unroll + u)

    loop(0, far_slots // unroll, term_group)
    for copy in tables:
        copy.wait()

    def owned(slab, chip, core):
        return terms_v[far_table_s[0, slab * leaves + chip * CORES + core]]

    def core_group(slab):
        for chip in range(chips):
            core_out_v[slab * chips + chip] = owned(slab, chip, 1 - my_core)

    for slab in range(slabs):
        core_group(slab)
    outward_core_copy().start()

    apex_row.wait()
    for t in range(slabs):
        apex2_v[t] = wide(apex_v[t])

    outward_core_copy().wait_recv()
    for slab in range(slabs):
        for chip in range(chips):
            k = slab * chips + chip
            slab_out_v[slab, chip] = (owned(slab, chip, my_core) + core_in_v[k]).astype(BF)
    loop(1, slabs, lambda k: outward_slab_copy(k).start())
    for chip in range(chips):
        own_v[chip] = owned(my_slab, chip, my_core) + core_in_v[my_slab * chips + chip]

    loop(1, leaves, lambda k: share_arrival(k).wait_recv())
    total = share_in_v[0]
    for j in range(1, leaves):
        total = total + share_in_v[j]
    slab_v[my_slab] = total
    loop(1, slabs, lambda k: slab_copy(k).start())

    loop(1, chips, lambda k: parent_chip_arrival(k).wait_recv())
    loop(1, slabs, lambda k: parent_slab_copy(k).start())

    @pl.when(me < devices - 1)
    def _():
        halo_copy(True).start()

    @pl.when(me > 0)
    def _():
        halo_copy(False).start()

    inputs[6].wait()

    def near_back(i, e0):
        left = masked_left_v[i]
        for w in range(width):
            collected_v[e0 + w] += nn(left, near_v[table_s[w, i]])

    def near_forward(i):
        blocks = jnp.concatenate([near_v[i * slots + s] for s in range(slots)], axis=1)
        picked = jnp.concatenate([ext_v[table_s[width + s, i]] for s in range(slots)], axis=1)
        near_out_v[i] = nt(picked, blocks)

    for i in range(HW):
        near_back(i, i + first * (HW - i))
    for i in range(clusters - HW, clusters):
        near_back(i, i - last * (i - (clusters - HW - 1)))

    edge_out_v[0] = collected_v[0:HW].astype(BF)
    edge_out_v[1] = collected_v[clusters + HW :].astype(BF)

    @pl.when(me < devices - 1)
    def _():
        edge_copy(True).start()

    @pl.when(me > 0)
    def _():
        edge_copy(False).start()

    def middle_back(g):
        i = HW + g * HW
        lefts = [masked_left_v[i + u] for u in range(HW)]
        for e in range(width + HW - 1):
            rows = [u for u in range(HW) if 0 <= e - u < width]
            left = jnp.concatenate([lefts[u] for u in rows], axis=1)
            blocks = jnp.concatenate([near_v[table_s[e - u, i + u]] for u in rows], axis=0)
            collected_v[i + e] += nn(left, blocks)

    middles = (clusters - 2 * HW) // HW
    loop(0, middles, middle_back)

    loop(1, slabs, lambda k: slab_arrival(k).wait_recv())

    def apex_products(product):
        total = jnp.zeros((chunk, lift_v.shape[1]), F32)
        for t in range(slabs):
            other = jnp.where(my_slab == t, 0.0, 1.0)
            total += product(slab_v[t] * other, apex2_v[t])
        top_v[my_leaf] = total

    @pl.when(is_right)
    def _():
        apex_products(three_nt)

    @pl.when(jnp.logical_not(is_right))
    def _():
        apex_products(three_nn)

    loop(1, leaves, lambda k: top_copy(k).start())

    loop(1, slabs, lambda k: outward_slab_arrival(k).wait_recv())
    for chip in range(chips):
        total = own_v[chip]
        for t in range(slabs):
            total = total + slab_in_v[t, chip].astype(F32)
        own_v[chip] = total
        chip_out_v[chip] = total.astype(BF)
    loop(1, chips, lambda k: outward_chip_copy(k).start())

    loop(1, slabs, lambda k: parent_slab_arrival(k).wait_recv())
    parent_core_copy().start()

    @pl.when(me > 0)
    def _():
        halo_copy(True).wait_recv()

    @pl.when(me < devices - 1)
    def _():
        halo_copy(False).wait_recv()

    def forward_group(g):
        for u in range(HW):
            near_forward(g * HW + u)

    loop(0, clusters // HW, forward_group)

    @pl.when(me > 0)
    def _():
        edge_copy(True).wait_recv()

    @pl.when(me < devices - 1)
    def _():
        edge_copy(False).wait_recv()

    collected_v[HW : 2 * HW] += edge_in_v[1].astype(F32)
    collected_v[clusters : clusters + HW] += edge_in_v[0].astype(F32)

    parent_core_arrival().wait_recv()
    batch = 4
    far_right = jnp.zeros((rhs, k2), F32)

    def far_group(g, total):
        chosen, pairs = [], []
        for u in range(batch):
            f = g * batch + u
            target = targets_s[f]
            at = spot(target // leaves, target % leaves)
            row = parents_v[jnp.where(f < count_s[0], at, CORES * group)]
            chosen += [row, row]
            pairs.append(coupling2_v[f])
        return total + nt(jnp.concatenate(chosen, axis=1), jnp.concatenate(pairs, axis=1))

    far_right = lax.fori_loop(0, far_slots // batch, far_group, far_right)

    loop(1, chips, lambda k: outward_chip_arrival(k).wait_recv())
    far_left = own_v[my_chip]
    for chip in range(chips):
        far_left = far_left + chip_in_v[chip].astype(F32)

    loop(1, leaves, lambda k: top_arrival(k).wait_recv())
    top = jnp.concatenate([top_v[j] for j in range(leaves)], axis=0)
    hat = three_nt(top, lift2_v[...]) + jnp.concatenate([far_right, far_left], axis=0)
    hat_ref[...] = paired_rows(hat)

    loop(1, leaves, lambda k: share_copy(k).wait_send())
    loop(1, leaves, lambda k: top_copy(k).wait_send())
    loop(1, slabs, lambda k: slab_copy(k).wait_send())
    loop(1, slabs, lambda k: parent_slab_copy(k).wait_send())
    loop(1, slabs, lambda k: outward_slab_copy(k).wait_send())
    loop(1, chips, lambda k: parent_chip_copy(k).wait_send())
    loop(1, chips, lambda k: outward_chip_copy(k).wait_send())
    parent_core_copy().wait_send()
    outward_core_copy().wait_send()

    @pl.when(me < devices - 1)
    def _():
        halo_copy(True).wait_send()
        edge_copy(True).wait_send()

    @pl.when(me > 0)
    def _():
        halo_copy(False).wait_send()
        edge_copy(False).wait_send()


def finish_kernel(
    pack,
    hat_ref,
    near_ref,
    back_ref,
    transfer_ref,
    basis_ref,
    keep_ref,
    product_h,
    adjoint_h,
    product_v,
    adjoint_v,
    sem,
):
    rhs = product_v.shape[0]
    rank = B // pack
    span = 2 * B
    pieces = transfer_ref.shape[0] // span
    lane2 = lax.broadcasted_iota(jnp.int32, (2 * rhs, B), 1)
    hat2 = hat_ref[...]
    copies = []
    for n in range(pieces):
        both = nt(hat2, transfer_ref[n * span : (n + 1) * span])
        down = (both[: 2 * rhs] + both[2 * rhs :]).astype(BF)
        for h in range(span // B):
            g = n * (span // B) + h
            piece = down[:, h * B : (h + 1) * B]
            rows = [
                jnp.where((lane2 >= u * rank) & (lane2 < (u + 1) * rank), piece, jnp.zeros_like(piece))
                for u in range(pack)
            ]
            out = nn(jnp.concatenate(rows, axis=0), basis_ref[g])
            for u in range(pack):
                c = g * pack + u
                keep = keep_ref[c : c + 1] > 0.0
                base = 2 * rhs * u
                window = slice(c * B, (c + 1) * B)
                product_v[:, window] = jnp.where(keep, near_ref[c] + out[base : base + rhs], 0.0)
                adjoint_v[:, window] = jnp.where(
                    keep, back_ref[c + HW] + out[base + rhs : base + 2 * rhs], 0.0
                )
        part = pl.ds(n * pack * span, pack * span)
        for i, (src, dst) in enumerate([(product_v, product_h), (adjoint_v, adjoint_h)]):
            copy = pltpu.make_async_copy(src.at[:, part], dst.at[:, part], sem.at[i, n])
            copy.start()
            copies.append(copy)
    for copy in copies:
        copy.wait()


def shards(
    right_sides,
    left_sides,
    near_blocks,
    near_columns,
    cluster_points,
    leaf_basis,
    transfer,
    far_parents,
    far_count,
    coupling,
    slab_transfer,
    apex_coupling,
):
    slabs, leaves = lax.axis_size("slab"), lax.axis_size("leaf")
    devices = slabs * leaves
    chips = leaves // CORES
    group = slabs * chips
    rhs, columns = right_sides.shape
    clusters, slots = near_columns.shape
    rank, k2 = transfer.shape[1:]
    k3 = slab_transfer.shape[2]
    far_slots = coupling.shape[1]
    width = 2 * HW + 1
    chunk = 2 * rhs // leaves
    pack = B // rank
    hbm = pl.BlockSpec(memory_space=pltpu.HBM)
    vmem = pl.BlockSpec(memory_space=pltpu.VMEM)
    dma = pltpu.SemaphoreType.DMA
    out = jax.ShapeDtypeStruct((rhs, columns), F32)
    held = pl.pallas_call(
        functools.partial(kernel, slabs, leaves),
        out_shape=(
            jax.ShapeDtypeStruct((4 * rhs, 2 * k2), BF),
            jax.ShapeDtypeStruct((clusters, rhs, B), F32),
            jax.ShapeDtypeStruct((clusters + 2 * HW, rhs, B), F32),
            jax.ShapeDtypeStruct((clusters * rank, 2 * k2), BF),
            jax.ShapeDtypeStruct((clusters // pack, B, B), BF),
            jax.ShapeDtypeStruct((clusters, B), F32),
        ),
        in_specs=[pl.BlockSpec(memory_space=pltpu.SMEM)] + [hbm] * 11,
        out_specs=(vmem,) * 6,
        scratch_shapes=[
            pltpu.VMEM((rhs, columns), BF),
            pltpu.VMEM((rhs, columns), BF),
            pltpu.VMEM((clusters * rank, k2), F32),
            pltpu.VMEM((k2, k3), F32),
            pltpu.VMEM(coupling.shape[1:], F32),
            pltpu.VMEM((slabs, k3, k3), F32),
            pltpu.VMEM((clusters * slots + 1, B, B), BF),
            pltpu.VMEM((slots, clusters), jnp.int32),
            pltpu.VMEM((width + slots, clusters), jnp.int32),
            pltpu.VMEM((1, devices), jnp.int32),
            pltpu.SMEM((clusters,), jnp.int32),
            pltpu.SMEM((far_slots,), jnp.int32),
            pltpu.SMEM((width + slots, clusters), jnp.int32),
            pltpu.SMEM((1, devices), jnp.int32),
            pltpu.VMEM((clusters + 2 * HW, rhs, B), BF),
            pltpu.VMEM((clusters, rhs, B), BF),
            pltpu.VMEM((4 * rhs, clusters * rank), BF),
            pltpu.VMEM((k2, 2 * k3), BF),
            pltpu.VMEM((far_slots, k2, 2 * k2), BF),
            pltpu.VMEM((slabs, k3, 2 * k3), BF),
            pltpu.VMEM((2, HW, rhs, B), BF),
            pltpu.VMEM((2, HW, rhs, B), BF),
            pltpu.VMEM((leaves, chunk, k3), F32),
            pltpu.VMEM((leaves, chunk, k3), F32),
            pltpu.VMEM((slabs, chunk, k3), F32),
            pltpu.VMEM((leaves, chunk, k3), F32),
            pltpu.VMEM((CORES * group + 1, rhs, k2), BF),
            pltpu.VMEM((far_slots + 1, rhs, k2), F32),
            pltpu.VMEM((group, rhs, k2), F32),
            pltpu.VMEM((group, rhs, k2), F32),
            pltpu.VMEM((slabs, chips, rhs, k2), BF),
            pltpu.VMEM((slabs, chips, rhs, k2), BF),
            pltpu.VMEM((chips, rhs, k2), F32),
            pltpu.VMEM((chips, rhs, k2), BF),
            pltpu.VMEM((chips, rhs, k2), BF),
            dma((11,)),
            dma((2,)),
            dma((2,)),
            dma((2,)),
            dma((2,)),
            dma((2,)),
            dma((leaves,)),
            dma((leaves,)),
            dma((slabs,)),
            dma((slabs,)),
            dma((leaves,)),
            dma((leaves,)),
            dma((chips,)),
            dma((chips,)),
            dma((slabs,)),
            dma((slabs,)),
            dma((chips,)),
            dma((chips,)),
            dma((slabs,)),
            dma((slabs,)),
            dma((2,)),
            dma((2,)),
        ],
        compiler_params=pltpu.CompilerParams(
            collective_id=0, has_side_effects=True, vmem_limit_bytes=50 * 1024 * 1024
        ),
        name="h2_step",
    )(
        far_count,
        *[
            pltpu.with_memory_space_constraint(array, pltpu.HBM)
            for array in (
                cluster_points,
                far_parents[0],
                near_columns.T,
                right_sides,
                left_sides,
                leaf_basis.reshape(clusters // pack, B, B),
                transfer.reshape(clusters * rank, k2),
                slab_transfer[0],
                coupling[0],
                apex_coupling,
                near_blocks.reshape(-1, B, B),
            )
        ],
    )
    pieces = clusters * rank // (2 * B)
    return pl.pallas_call(
        functools.partial(finish_kernel, pack),
        out_shape=(out, out),
        in_specs=[vmem] * 6,
        out_specs=(hbm, hbm),
        scratch_shapes=[
            pltpu.VMEM((rhs, columns), F32),
            pltpu.VMEM((rhs, columns), F32),
            dma((2, pieces)),
        ],
        compiler_params=pltpu.CompilerParams(vmem_limit_bytes=8 * 1024 * 1024),
        name="h2_finish",
    )(*held)


def solution(mesh):
    return jax.shard_map(
        shards,
        mesh=mesh,
        in_specs=(
            P(None, ("slab", "leaf")),
            P(None, ("slab", "leaf")),
            P(("slab", "leaf"), None, None, None),
            P(("slab", "leaf"), None),
            P(("slab", "leaf")),
            P(("slab", "leaf"), None, None),
            P(("slab", "leaf"), None, None),
            P(("slab", "leaf"), None),
            P(("slab", "leaf")),
            P(("slab", "leaf"), None, None, None),
            P(("slab", "leaf"), None, None),
            P(),
        ),
        out_specs=(P(None, ("slab", "leaf")), P(None, ("slab", "leaf"))),
        check_vma=False,
    )
```
